32 devices in a mesh: row: 8 (over y, x, core), col: 4 (over z).
Axes of the slice: x: 2, y: 2, z: 4, core: 2. Of those that a mesh axis runs over, the one named last changes fastest.
Arguments:
- pair_in: bfloat16 [384, 384, 128], P('row', 'col'), may hold values from -6 to 6
- coords: float32 [3, 384], P(None, 'row'), may hold values from -36 to 36
- chain_ids: int32 [384], P('row'), may hold values from 0 to 3, never falling along the last dimension, each value on 1 to 192 neighbouring positions
- coord_mask: int32 [384], P('row'), may hold values 0 or 1
- gain_tri: float32 [128], replicated, may hold values from 0.1 to 1.9
- gain_sum: float32 [128], replicated, may hold values from 0.1 to 1.9
- gain_attn: float32 [128], replicated, may hold values from 0.1 to 1.9
- w_tri_in: bfloat16 [128, 640], replicated, may hold values from -0.5 to 0.5
- w_tri_out: bfloat16 [128, 128], replicated, may hold values from -0.5 to 0.5
- w_bins: float32 [36, 128], replicated, may hold values from -3 to 3
- same_chain: float32 [128], replicated, may hold values from -6 to 6
- w_query: bfloat16 [128, 128], replicated, may hold values from -8 to 8
- w_attn: bfloat16 [128, 384], replicated, may hold values from -0.5 to 0.5
- w_bias: bfloat16 [128, 4], replicated, may hold values from -0.5 to 0.5
- w_attn_out: bfloat16 [128, 128], replicated, may hold values from -0.5 to 0.5
Outputs:
- pair_out: bfloat16 [384, 384, 128], P('row', 'col')
The draws below stay inside these ranges and needn't reach their ends.
Inputs may be any that keep to these rules, and one draw needn't show every extreme that they name: `chain_ids`: chain numbers never fall along the residues, and no chain holds more than half of them.
All inputs are finite; a program needn't handle non-finite values. No bound on the sum of `coord_mask` on one device may be relied on, other than what follows from the above.
Results may differ from the reference program's by a relative error of at most 0.02.
Values may be sent and summed in bfloat16 or wider, within the bound.
A program may use at most 192 MiB of HBM per device.

```python
import math
import jax
import jax.numpy as jnp
import numpy as np
from jax import lax

CP = 128
HEADS = 4
HEAD_DIM = 32
NBINS = 36
L = 384


def draw_w_query(key, part):
    first_key = jax.random.fold_in(key, 11)
    second_key = jax.random.fold_in(key, 12)
    base = jnp.clip(jax.random.normal(first_key, (CP, CP), jnp.float32), -4.0, 4.0) * CP ** (-0.5)
    factor = jnp.exp(jax.random.uniform(second_key, (HEADS,), jnp.float32, jnp.log(0.5), jnp.log(2.0)))
    scaled = base * jnp.repeat(factor, CP // HEADS)[None, :]
    return jnp.clip(scaled, -8.0, 8.0).astype(jnp.bfloat16)


def with_ends(values, rng, least, top_value):
    shape = values.shape
    index_at = [jax.random.randint(jax.random.fold_in(rng, axis), (), 0, shape[axis]) for axis in range(len(shape))]
    values = values.at[tuple(index_at)].set(least)
    longest = shape.index(max(shape))
    index_at[longest] = (index_at[longest] + 1) % shape[longest]
    return values.at[tuple(index_at)].set(top_value)


def block_scale(rng, shape, pieces, smallest, largest):
    def one(axis_at, parts):
        steps = jax.random.uniform(jax.random.fold_in(jax.random.fold_in(rng, 6), axis_at), (parts,), jnp.float32, smallest / len(pieces), largest / len(pieces))
        return jnp.repeat(jnp.exp(steps), shape[axis_at] // parts).reshape((-1,) + (1,) * (len(shape) - axis_at - 1))

    loudness = one(*pieces[0])
    for cut in pieces[1:]:
        loudness = loudness * one(*cut)
    return loudness


def profile(count, total, reach, lean):
    loads = [(1 << 20) // math.isqrt(standing ** lean) + 1 for standing in range(2, count + 1)]
    spare, holding = total - reach - (count - 1), [1] * (count - 1)
    while spare > 0:
        movable = [i for i in range(count - 1) if holding[i] < reach]
        pool, remaining = sum([loads[i] for i in movable]), spare
        for i in movable:
            extra = min(reach - holding[i], max(1, remaining * loads[i] // pool), spare)
            holding[i] = holding[i] + extra
            spare = spare - extra
    return np.array([reach] + holding)


def ragged(key, count, total, limit, skew):
    if count == 2:
        one = jax.random.randint(key, (), max(1, total - limit), min(limit, total - 1) + 1)
        return jnp.stack([one, total - one])
    lengths = jnp.asarray(profile(count, total, limit, skew), jnp.int32)
    pairs = (count - 1) // 2
    donor, receiver = lengths[1:1 + 2 * pairs:2], lengths[2:2 + 2 * pairs:2]
    room = jnp.minimum(donor - 1, limit - receiver)
    moved = jax.random.randint(jax.random.fold_in(key, 1), (pairs,), 0, 1 << 20) % (room + 1)
    lengths = lengths.at[1:1 + 2 * pairs:2].set(donor - moved).at[2:2 + 2 * pairs:2].set(receiver + moved)
    return lengths[jax.random.permutation(jax.random.fold_in(key, 2), count)]


def scatter_about(stream_key, shape, scale, most, shards=(), kind=jnp.bfloat16):
    level = block_scale(stream_key, shape, shards, -0.22, 0.18) if shards else 1.0
    values = jax.random.normal(stream_key, shape, jnp.float32) * scale * level
    return jnp.minimum(jnp.maximum(values, -most), most).astype(kind)


def setup_inputs(seed: int = 0) -> dict:
    streams_of = jax.random.split(jax.random.key(seed), 16)
    return {
        "pair_in": scatter_about(streams_of[0], (L, L, CP), 1.0, 6.0, ((0, 8), (1, 4))),
        "coords": scatter_about(streams_of[1], (3, L), 6.0, 36.0, ((1, 8),), jnp.float32),
        "chain_ids": jnp.searchsorted(jnp.cumsum(ragged(streams_of[2], 4, L, L // 2, 0)), jnp.arange(L), side="right").astype(jnp.int32),
        "coord_mask": with_ends((jax.random.randint(streams_of[3], (L,), 0, 8) < 7).astype(jnp.int32), jax.random.fold_in(streams_of[3], 1), 0, 1),
        "gain_tri": jnp.clip(1.0 + 0.18 * jax.random.normal(streams_of[4], (CP,), jnp.float32), 0.1, 1.9),
        "gain_sum": jnp.clip(1.0 + 0.18 * jax.random.normal(streams_of[5], (CP,), jnp.float32), 0.1, 1.9),
        "gain_attn": jnp.clip(1.0 + 0.18 * jax.random.normal(streams_of[6], (CP,), jnp.float32), 0.1, 1.9),
        "w_tri_in": scatter_about(streams_of[7], (CP, 5 * CP), CP ** -0.5, 0.5),
        "w_tri_out": scatter_about(streams_of[8], (CP, CP), CP ** -0.5, 0.5),
        "w_bins": scatter_about(streams_of[9], (NBINS, CP), 0.5, 3.0, (), jnp.float32),
        "same_chain": scatter_about(streams_of[10], (CP,), 1.0, 6.0, (), jnp.float32),
        "w_query": draw_w_query(jax.random.fold_in(streams_of[15], 71), 0),
        "w_attn": scatter_about(streams_of[12], (CP, 3 * CP), CP ** -0.5, 0.5),
        "w_bias": scatter_about(streams_of[13], (CP, HEADS), CP ** -0.5, 0.5),
        "w_attn_out": scatter_about(streams_of[14], (CP, CP), CP ** -0.5, 0.5),
    }


def layer_norm(values, gain):
    center = values - lax.optimization_barrier(jnp.mean(values, axis=-1, keepdims=True))
    spread = lax.optimization_barrier(jnp.mean(center * center, axis=-1, keepdims=True))
    return center * lax.rsqrt(spread + 1e-05) * gain

def reference(pair_in, coords, chain_ids, coord_mask, gain_tri, gain_sum, gain_attn, w_tri_in, w_tri_out, w_bins, same_chain, w_query, w_attn, w_bias, w_attn_out):
    pair_wide = pair_in.astype(jnp.float32)
    normed = layer_norm(pair_wide, gain_tri).astype(jnp.bfloat16)
    projected = jnp.dot(normed.reshape(L * L, CP), w_tri_in, preferred_element_type=jnp.float32).reshape(L, L, 5 * CP)
    left_side = (jax.nn.sigmoid(projected[..., :CP]) * projected[..., CP:2 * CP]).astype(jnp.bfloat16)
    right_side = (jax.nn.sigmoid(projected[..., 2 * CP:3 * CP]) * projected[..., 3 * CP:4 * CP]).astype(jnp.bfloat16)
    tri_gate = jax.nn.sigmoid(projected[..., 4 * CP:])
    left_first = left_side.astype(jnp.float32).transpose(2, 0, 1)
    right_first = right_side.astype(jnp.float32).transpose(2, 0, 1)
    product = jnp.einsum('cik,cjk->cij', left_first, right_first).transpose(1, 2, 0)
    summed_norm = layer_norm(product, gain_sum).astype(jnp.bfloat16)
    pair_one = pair_wide + tri_gate * jnp.dot(summed_norm.reshape(L * L, CP), w_tri_out, preferred_element_type=jnp.float32).reshape(L, L, CP)
    offsets = coords[:, :, None] - coords[:, None, :]
    dist = jnp.sqrt(lax.optimization_barrier(jnp.sum(offsets * offsets, axis=0)) + 1.0)
    centres = 2.0 + 20.0 * jnp.arange(NBINS, dtype=jnp.float32) / (NBINS - 1)
    spacing = 25.0 / (NBINS - 1)
    present = coord_mask.astype(jnp.float32)
    pair_mask = present[:, None] * present[None, :]
    feats = jnp.exp(-((dist[..., None] - centres) / spacing) ** 2) * pair_mask[..., None]
    binned = jnp.dot(feats.reshape(L * L, NBINS), w_bins, precision=lax.Precision.HIGHEST).reshape(L, L, CP)
    shared = (chain_ids[:, None] == chain_ids[None, :]).astype(jnp.float32)
    pair_two = (pair_one + binned + shared[..., None] * same_chain).astype(jnp.bfloat16)
    normed_two = layer_norm(pair_two.astype(jnp.float32), gain_attn).astype(jnp.bfloat16)
    flat_two = normed_two.reshape(L * L, CP)
    queries = jnp.dot(flat_two, w_query, preferred_element_type=jnp.float32).astype(jnp.bfloat16).reshape(L, L, HEADS, HEAD_DIM)
    rest = jnp.dot(flat_two, w_attn, preferred_element_type=jnp.float32).reshape(L, L, 3 * CP)
    key_rows = rest[..., :CP].astype(jnp.bfloat16).reshape(L, L, HEADS, HEAD_DIM)
    value_rows = rest[..., CP:2 * CP].astype(jnp.bfloat16).reshape(L, L, HEADS, HEAD_DIM)
    attn_gate = jax.nn.sigmoid(rest[..., 2 * CP:])
    pair_bias = jnp.dot(flat_two, w_bias, preferred_element_type=jnp.float32).astype(jnp.bfloat16).reshape(L, L, HEADS)
    bias_first = pair_bias.astype(jnp.float32).transpose(2, 0, 1)
    group = math.gcd(L, 16)
    blocks = L // group

    def one_block(items):
        query_blk, key_blk, value_blk = items
        scores = jnp.einsum('ijhd,ikhd->ihjk', query_blk.astype(jnp.float32), key_blk.astype(jnp.float32)) / math.sqrt(HEAD_DIM) + bias_first[None]
        top = lax.optimization_barrier(jnp.max(scores, axis=-1, keepdims=True))
        expo = jnp.exp(scores - top)
        weights = lax.optimization_barrier(expo.astype(jnp.bfloat16)).astype(jnp.float32)
        numer = jnp.einsum('ihjk,ikhd->ihjd', weights, value_blk.astype(jnp.float32))
        return numer / lax.optimization_barrier(jnp.sum(expo, axis=-1))[..., None]
    attended = lax.map(one_block, (queries.reshape(blocks, group, L, HEADS, HEAD_DIM), key_rows.reshape(blocks, group, L, HEADS, HEAD_DIM), value_rows.reshape(blocks, group, L, HEADS, HEAD_DIM)))
    attended = attended.reshape(L, HEADS, L, HEAD_DIM).transpose(0, 2, 1, 3).reshape(L, L, CP)
    gated = (attn_gate * attended).astype(jnp.bfloat16)
    result = pair_two.astype(jnp.float32) + jnp.dot(gated.reshape(L * L, CP), w_attn_out, preferred_element_type=jnp.float32).reshape(L, L, CP)
    return result.astype(jnp.bfloat16)
```

```python
import functools
import math

import jax
import jax.numpy as jnp
from jax import lax
from jax.experimental import pallas as pl
from jax.experimental.pallas import tpu as pltpu
from jax.sharding import PartitionSpec as P

MESH = pl.DeviceIdType.MESH
LOG2E = math.log2(math.e)
PIECES = 2


def contract_last(a, b):
    return lax.dot_general(a, b, (((1,), (1,)), ((), ())), preferred_element_type=jnp.float32)


def attend_kernel(
    n_row,
    n_col,
    n_heads,
    normed_ref,
    bias_ref,
    pair_ref,
    wq_ref,
    wk_ref,
    wvt_ref,
    wg_ref,
    wo_ref,
    out_ref,
    blocks,
    land,
    bias_all,
    bias_full,
    q_wide,
    top,
    total,
    acc,
    hop1_send,
    hop1_recv,
    hop2_send,
    hop2_recv,
    hop3_send,
    hop3_recv,
    copy_sem,
    right_send,
    left_send,
    block_recv,
):
    row = lax.axis_index("row")
    col = lax.axis_index("col")
    rows, cols, channels = normed_ref.shape
    halves = cols // rows
    head = channels // n_heads
    wide = cols * n_heads
    strip = rows * n_heads
    core = lax.rem(row, halves)
    home = row // halves
    groups = n_row // halves
    part = rows // PIECES

    barrier = pltpu.get_barrier_semaphore()
    for step in range(1, n_row):
        pl.semaphore_signal(
            barrier, inc=1, device_id=(lax.rem(row + step, n_row), col), device_id_type=MESH
        )
    for step in range(1, n_col):
        pl.semaphore_signal(
            barrier, inc=1, device_id=(row, lax.rem(col + step, n_col)), device_id_type=MESH
        )
    pl.semaphore_wait(barrier, n_row - 1 + n_col - 1)

    def hop1(source):
        return pltpu.make_async_remote_copy(
            src_ref=bias_ref,
            dst_ref=land.at[source],
            send_sem=hop1_send,
            recv_sem=hop1_recv.at[source],
            device_id=(row, home),
            device_id_type=MESH,
        )

    @pl.when(col != home)
    def _():
        hop1(col).start()

    def piece_copy(owner, piece, own, to_right):
        at = pl.ds(piece * part, part)
        source = normed_ref.at[at] if own else blocks.at[owner, at]
        sems = right_send if to_right else left_send
        return pltpu.make_async_remote_copy(
            src_ref=source,
            dst_ref=blocks.at[owner, at],
            send_sem=sems.at[owner, piece],
            recv_sem=block_recv.at[owner, piece],
            device_id=(row, col + 1 if to_right else col - 1),
            device_id_type=MESH,
        )

    for piece in range(PIECES):

        @pl.when(col < n_col - 1)
        def _():
            piece_copy(col, piece, True, True).start()

        @pl.when(col > 0)
        def _():
            piece_copy(col, piece, True, False).start()

    lane = lax.broadcasted_iota(jnp.int32, (rows, channels), 1) // head

    def make_queries(i, carry):
        query = jnp.dot(normed_ref[i], wq_ref[...], preferred_element_type=jnp.float32)
        for half in range(halves):
            mine = query[half * rows : (half + 1) * rows]
            for h in range(n_heads):
                start = half * strip + h * rows
                q_wide[i, start : start + rows, :] = jnp.where(lane == h, mine, 0.0).astype(
                    jnp.bfloat16
                )
        return carry

    lax.fori_loop(0, rows, make_queries, 0, unroll=2)

    def hop2(step):
        return pltpu.make_async_remote_copy(
            src_ref=land,
            dst_ref=bias_all.at[core],
            send_sem=hop2_send.at[step],
            recv_sem=hop2_recv,
            device_id=(lax.rem(home + step, groups) * halves + core, col),
            device_id_type=MESH,
        )

    def hop3(slot):
        return pltpu.make_async_remote_copy(
            src_ref=bias_all.at[slot],
            dst_ref=bias_all.at[slot],
            send_sem=hop3_send,
            recv_sem=hop3_recv,
            device_id=(home * halves + (1 - core), col),
            device_id_type=MESH,
        )

    @pl.when(col == home)
    def _():
        own = pltpu.make_async_copy(bias_ref, land.at[col], copy_sem)
        own.start()
        own.wait()
        for step in range(1, n_col):
            hop1(lax.rem(col + step, n_col)).wait_recv()
        for step in range(1, groups):
            hop2(step).start()
        keep = pltpu.make_async_copy(land, bias_all.at[core], copy_sem)
        keep.start()
        keep.wait()

    @pl.when(col != home)
    def _():
        hop2(1).wait_recv()

    hop3(core).start()
    hop3(1 - core).wait_recv()

    for k in range(n_col):
        for half in range(halves):
            bias_full[k, :, half * strip : (half + 1) * strip] = (
                bias_all[half, k].astype(jnp.float32) * LOG2E
            )

    lane_head = lax.rem(lax.broadcasted_iota(jnp.int32, (head, wide), 1), strip) // rows
    factor = LOG2E / math.sqrt(head)

    def attend(block, owner, i, first):
        keys = jnp.dot(block, wk_ref[...], preferred_element_type=jnp.float32).astype(jnp.bfloat16)
        values = contract_last(wvt_ref[...], block).astype(jnp.bfloat16)
        scores = contract_last(keys, q_wide[i]) * factor + bias_full[owner]
        peak = jnp.max(scores, axis=0, keepdims=True)
        if not first:
            old = top[i]
            peak = jnp.maximum(old, peak)
            shrink = jnp.exp2(old - peak)
        expo = jnp.exp2(scores - peak)
        summed = jnp.sum(expo, axis=0, keepdims=True)
        mixed = jnp.dot(values, expo.astype(jnp.bfloat16), preferred_element_type=jnp.float32)
        picked = mixed[:head]
        for h in range(1, n_heads):
            picked = jnp.where(lane_head == h, mixed[h * head : (h + 1) * head], picked)
        top[i] = peak
        if first:
            total[i] = summed
            acc[i] = picked
        else:
            total[i] = total[i] * shrink + summed
            acc[i] = acc[i] * shrink + picked

    def own_rows(i, carry):
        attend(normed_ref[i], col, i, True)
        return carry

    lax.fori_loop(0, rows, own_rows, 0, unroll=2)

    def arrived(step, carry):
        low, high = col - step, col + step
        for piece in range(PIECES):

            def rows_of(owner):
                def one(n, carry):
                    i = piece * part + n
                    attend(blocks[owner, i], owner, i, False)
                    return carry

                lax.fori_loop(0, part, one, 0, unroll=2)

            @pl.when(low >= 0)
            def _():
                piece_copy(low, piece, False, True).wait_recv()

                @pl.when(col < n_col - 1)
                def _():
                    piece_copy(low, piece, False, True).start()

            @pl.when(high < n_col)
            def _():
                piece_copy(high, piece, False, False).wait_recv()

                @pl.when(col > 0)
                def _():
                    piece_copy(high, piece, False, False).start()

            @pl.when(low >= 0)
            def _():
                rows_of(low)

            @pl.when(high < n_col)
            def _():
                rows_of(high)

        return carry

    lax.fori_loop(1, n_col, arrived, 0)

    def finish(i, carry):
        gate = jax.nn.sigmoid(
            jnp.dot(normed_ref[i], wg_ref[...], preferred_element_type=jnp.float32)
        )
        mean = acc[i] / total[i]
        stacked = jnp.concatenate(
            [
                jnp.concatenate(
                    [
                        mean[:, half * strip + h * rows : half * strip + (h + 1) * rows]
                        for half in range(halves)
                    ],
                    axis=1,
                )
                for h in range(n_heads)
            ],
            axis=0,
        )
        gated = (gate * stacked.T).astype(jnp.bfloat16)
        out_ref[i] = (
            pair_ref[i].astype(jnp.float32)
            + jnp.dot(gated, wo_ref[...], preferred_element_type=jnp.float32)
        ).astype(jnp.bfloat16)
        return carry

    lax.fori_loop(0, rows, finish, 0, unroll=2)

    @pl.when(col != home)
    def _():
        hop1(col).wait_send()

    @pl.when(col == home)
    def _():
        for step in range(1, groups):
            hop2(step).wait_send()

    hop3(core).wait_send()
    for piece in range(PIECES):
        for owner in range(n_col):

            @pl.when((owner <= col) & (col < n_col - 1))
            def _():
                piece_copy(owner, piece, False, True).wait_send()

            @pl.when((owner >= col) & (col > 0))
            def _():
                piece_copy(owner, piece, False, False).wait_send()


def attend(n_row, n_col, n_heads, normed, bias, pair, wq, wk, wvt, wg, wo):
    rows, cols, channels = normed.shape
    halves = cols // rows
    assert halves == 2 and cols % rows == 0 and n_row % 2 == 0
    groups = n_row // halves
    wide = cols * n_heads
    dma = pltpu.SemaphoreType.DMA
    vmem = pl.BlockSpec(memory_space=pltpu.VMEM)
    return pl.pallas_call(
        functools.partial(attend_kernel, n_row, n_col, n_heads),
        out_shape=jax.ShapeDtypeStruct(normed.shape, jnp.bfloat16),
        in_specs=[vmem] * 8,
        out_specs=vmem,
        scratch_shapes=[
            pltpu.VMEM((n_col,) + normed.shape, jnp.bfloat16),
            pltpu.VMEM((n_col,) + bias.shape, jnp.bfloat16),
            pltpu.VMEM((halves, n_col) + bias.shape, jnp.bfloat16),
            pltpu.VMEM((n_col, cols, wide), jnp.float32),
            pltpu.VMEM((rows, wide, channels), jnp.bfloat16),
            pltpu.VMEM((rows, 1, wide), jnp.float32),
            pltpu.VMEM((rows, 1, wide), jnp.float32),
            pltpu.VMEM((rows, channels // n_heads, wide), jnp.float32),
            dma,
            dma((n_col,)),
            dma((groups,)),
            dma,
            dma,
            dma,
            dma,
            dma((n_col, PIECES)),
            dma((n_col, PIECES)),
            dma((n_col, PIECES)),
        ],
        compiler_params=pltpu.CompilerParams(
            collective_id=1, has_side_effects=True, vmem_limit_bytes=48 * 2**20
        ),
        name="attend",
    )(normed, bias, pair, wq, wk, wvt, wg, wo)


def layer_norm(values, gain):
    center = values - jnp.mean(values, axis=-1, keepdims=True)
    spread = jnp.mean(center * center, axis=-1, keepdims=True)
    return center * lax.rsqrt(spread + 1e-05) * gain


def body(
    pair_in,
    coords,
    chain_ids,
    coord_mask,
    gain_tri,
    gain_sum,
    gain_attn,
    w_tri_in,
    w_tri_out,
    w_bins,
    same_chain,
    w_query,
    w_attn,
    w_bias,
    w_attn_out,
):
    row_count, col_count, channels = pair_in.shape
    n_heads = w_bias.shape[1]
    n_bins = w_bins.shape[0]
    col_start = lax.axis_index("col") * col_count
    coords_all, chains_all, masks_all = (
        lax.all_gather(coords, "row", axis=1, tiled=True),
        lax.all_gather(chain_ids, "row", axis=0, tiled=True),
        lax.all_gather(coord_mask, "row", axis=0, tiled=True),
    )
    pair_wide = pair_in.astype(jnp.float32)
    normed = layer_norm(pair_wide, gain_tri).astype(jnp.bfloat16)
    projected = jnp.dot(
        normed.reshape(row_count * col_count, channels),
        w_tri_in,
        preferred_element_type=jnp.float32,
    ).reshape(row_count, col_count, 5 * channels)
    left_side = (
        (jax.nn.sigmoid(projected[..., :channels]) * projected[..., channels : 2 * channels])
        .astype(jnp.bfloat16)
        .transpose(2, 0, 1)
    )
    right_side = (
        (
            jax.nn.sigmoid(projected[..., 2 * channels : 3 * channels])
            * projected[..., 3 * channels : 4 * channels]
        )
        .astype(jnp.bfloat16)
        .transpose(2, 0, 1)
    )
    tri_gate = jax.nn.sigmoid(projected[..., 4 * channels :])
    right_cols = lax.all_gather(right_side, "row", axis=1, tiled=True)
    summed = lax.psum_scatter(
        jnp.einsum(
            "cjk,cik->jci", right_cols, left_side, preferred_element_type=jnp.float32
        ).astype(jnp.bfloat16),
        "col",
        scatter_dimension=0,
        tiled=True,
    )
    product = summed.transpose(2, 0, 1).astype(jnp.float32)
    summed_norm = layer_norm(product, gain_sum).astype(jnp.bfloat16)
    pair_one = pair_wide + tri_gate * jnp.dot(
        summed_norm.reshape(row_count * col_count, channels),
        w_tri_out,
        preferred_element_type=jnp.float32,
    ).reshape(row_count, col_count, channels)
    far_coords = lax.dynamic_slice_in_dim(coords_all, col_start, col_count, 1)
    far_chains = lax.dynamic_slice_in_dim(chains_all, col_start, col_count, 0)
    far_masks = lax.dynamic_slice_in_dim(masks_all, col_start, col_count, 0)
    offsets = coords[:, :, None] - far_coords[:, None, :]
    dist = jnp.sqrt(jnp.sum(offsets * offsets, axis=0) + 1.0)
    centres = 2.0 + 20.0 * jnp.arange(n_bins, dtype=jnp.float32) / (n_bins - 1)
    spacing = 25.0 / (n_bins - 1)
    pair_mask = coord_mask.astype(jnp.float32)[:, None] * far_masks.astype(jnp.float32)[None, :]
    feats = jnp.exp(-(((dist[..., None] - centres) / spacing) ** 2)) * pair_mask[..., None]
    binned = jnp.dot(
        feats.reshape(row_count * col_count, n_bins), w_bins, precision=lax.Precision.HIGHEST
    ).reshape(row_count, col_count, channels)
    shared = (chain_ids[:, None] == far_chains[None, :]).astype(jnp.float32)
    pair_two = (pair_one + binned + shared[..., None] * same_chain).astype(jnp.bfloat16)
    normed_two = layer_norm(pair_two.astype(jnp.float32), gain_attn).astype(jnp.bfloat16)
    flat_two = normed_two.reshape(row_count * col_count, channels)
    pair_bias = (
        jnp.dot(flat_two, w_bias, preferred_element_type=jnp.float32)
        .astype(jnp.bfloat16)
        .reshape(row_count, col_count, n_heads)
        .transpose(1, 2, 0)
        .reshape(col_count, n_heads * row_count)
    )
    return attend(
        lax.axis_size("row"),
        lax.axis_size("col"),
        n_heads,
        normed_two,
        pair_bias,
        pair_two,
        w_query,
        w_attn[:, :channels],
        w_attn[:, channels : 2 * channels].T,
        w_attn[:, 2 * channels :],
        w_attn_out,
    )


def solution(mesh):
    return jax.shard_map(
        body,
        mesh=mesh,
        in_specs=(
            P("row", "col", None),
            P(None, "row"),
            P("row"),
            P("row"),
            P(),
            P(),
            P(),
            P(),
            P(),
            P(),
            P(),
            P(),
            P(),
            P(),
            P(),
        ),
        out_specs=P("row", "col", None),
        check_vma=False,
    )
```

```python
import functools
import math

import jax
import jax.numpy as jnp
from jax import lax
from jax.experimental import pallas as pl
from jax.experimental.pallas import tpu as pltpu
from jax.sharding import PartitionSpec as P

MESH = pl.DeviceIdType.MESH
LOG2E = math.log2(math.e)
PIECES = 2


def contract_last(a, b):
    return lax.dot_general(a, b, (((1,), (1,)), ((), ())), preferred_element_type=jnp.float32)


CHUNKS = 4


def flip(index, bit):
    return index + bit - 2 * bit * lax.rem(index // bit, 2)


def routes(bits):
    found = []
    for offset in range(2, sum(bits) + 2, 2):
        used = [n for n, bit in enumerate(bits) if offset & bit]
        found.append((len(used), offset, bits[used[-1] + 1 :]))
    return [(offset, later) for _, offset, later in sorted(found)]


def triangle_kernel(
    n_row,
    n_col,
    pack,
    left_ref,
    right_ref,
    out_ref,
    gathered,
    left_wide,
    sums,
    land,
    own_sem,
    hop_send,
    hop_recv,
    up_send,
    down_send,
    sum_recv,
):
    row = lax.axis_index("row")
    col = lax.axis_index("col")
    groups, rows, depth = left_ref.shape
    chunk = groups // CHUNKS
    cols = depth // pack
    halves = cols // rows
    core = lax.rem(row, 2)
    bits = [1 << n for n in range(1, n_row.bit_length() - 1)]
    orders = (bits, bits[::-1])

    barrier = pltpu.get_barrier_semaphore()
    for step in range(1, n_row):
        pl.semaphore_signal(
            barrier, inc=1, device_id=(lax.rem(row + step, n_row), col), device_id_type=MESH
        )
    for step in range(1, n_col):
        pl.semaphore_signal(
            barrier, inc=1, device_id=(row, lax.rem(col + step, n_col)), device_id_type=MESH
        )
    pl.semaphore_wait(barrier, n_row - 1 + n_col - 1)

    def hop(source, part, bit, own=False):
        at = pl.ds(part * chunk, chunk)
        return pltpu.make_async_remote_copy(
            src_ref=right_ref.at[at] if own else gathered.at[source, at],
            dst_ref=gathered.at[source, at],
            send_sem=hop_send.at[bit.bit_length() - 1, source, part],
            recv_sem=hop_recv.at[source, part],
            device_id=(flip(row, bit), col),
            device_id_type=MESH,
        )

    for part in range(CHUNKS):
        for bit in bits + [1]:
            hop(row, part, bit, True).start()
    own_copy = pltpu.make_async_copy(right_ref, gathered.at[row], own_sem)
    own_copy.start()

    lane = lax.broadcasted_iota(jnp.int32, (rows, depth), 1) // cols

    def widen(g, carry):
        mine = left_ref[g].astype(jnp.float32)
        for a in range(pack):
            left_wide[g, a * rows : (a + 1) * rows, :] = jnp.where(lane == a, mine, 0.0).astype(
                jnp.bfloat16
            )
        return carry

    lax.fori_loop(0, groups, widen, 0)
    own_copy.wait()

    def source_of(offset):
        source = row
        for bit in bits + [1]:
            if offset & bit:
                source = flip(source, bit)
        return source

    def forward(part):
        for parity in range(2):

            @pl.when(core == parity)
            def _():
                for offset, later in routes(orders[parity]):
                    source = source_of(offset)
                    hop(source, part, 1).wait_recv()
                    for bit in later + [1]:
                        hop(source, part, bit).start()

    def send_sum(dest, part, up):
        at = pl.ds(part * chunk, chunk)
        return pltpu.make_async_remote_copy(
            src_ref=sums.at[dest, at],
            dst_ref=land.at[dest + 1 if up else dest, at],
            send_sem=(up_send if up else down_send).at[dest, part],
            recv_sem=sum_recv.at[dest + 1 if up else dest, part],
            device_id=(row, col + 1 if up else col - 1),
            device_id_type=MESH,
        )

    def add_landed(dest, part, up):
        send_sum(dest, part, up).wait_recv()
        slot = dest + 1 if up else dest

        def one(n, carry):
            g = part * chunk + n
            sums[dest, g] = (
                sums[dest, g].astype(jnp.float32) + land[slot, g].astype(jnp.float32)
            ).astype(jnp.bfloat16)
            return carry

        lax.fori_loop(0, chunk, one, 0)

    forward(0)
    for part in range(CHUNKS):
        for offset in range(1, n_row, 2):
            hop(source_of(offset), part, 1).wait_recv()

        def partial(n, carry):
            dest, g = n // chunk, part * chunk + lax.rem(n, chunk)
            far = jnp.concatenate(
                [gathered[dest * halves + half, g] for half in range(halves)], axis=0
            )
            sums[dest, g] = contract_last(far, left_wide[g]).astype(jnp.bfloat16)
            return carry

        lax.fori_loop(0, n_col * chunk, partial, 0)

        @pl.when(col == 0)
        def _():
            for dest in range(n_col - 1, 0, -1):
                send_sum(dest, part, True).start()

        @pl.when(col == n_col - 1)
        def _():
            for dest in range(n_col - 1):
                send_sum(dest, part, False).start()

        if part + 1 < CHUNKS:
            forward(part + 1)

        for step in range(1, n_col):
            high, low = n_col - step, step - 1

            @pl.when((col < high) & (col > 0))
            def _():
                add_landed(high, part, True)
                send_sum(high, part, True).start()

            @pl.when((col > low) & (col < n_col - 1))
            def _():
                add_landed(low, part, False)
                send_sum(low, part, False).start()

        @pl.when(col > 0)
        def _():
            add_landed(col, part, True)

        @pl.when(col < n_col - 1)
        def _():
            add_landed(col, part, False)

    def store(g, carry):
        out_ref[g] = sums[col, g]
        return carry

    lax.fori_loop(0, groups, store, 0)

    for part in range(CHUNKS):
        for bit in bits + [1]:
            hop(row, part, bit, True).wait_send()
        for parity in range(2):

            @pl.when(core == parity)
            def _():
                for offset, later in routes(orders[parity]):
                    for bit in later + [1]:
                        hop(source_of(offset), part, bit).wait_send()

        for dest in range(n_col):

            @pl.when(col < dest)
            def _():
                send_sum(dest, part, True).wait_send()

            @pl.when(col > dest)
            def _():
                send_sum(dest, part, False).wait_send()


def triangle(n_row, n_col, left, right):
    rows, cols, channels = left.shape
    pack = 128 // math.gcd(rows, 128)
    groups = channels // pack
    assert cols == 2 * rows and groups % CHUNKS == 0 and n_row & (n_row - 1) == 0

    def packed(side):
        return (
            side.reshape(rows, cols, pack, groups)
            .transpose(3, 0, 2, 1)
            .reshape(groups, rows, pack * cols)
        )

    dma = pltpu.SemaphoreType.DMA
    vmem = pl.BlockSpec(memory_space=pltpu.VMEM)
    block = (groups, cols, pack * rows)
    summed = pl.pallas_call(
        functools.partial(triangle_kernel, n_row, n_col, pack),
        out_shape=jax.ShapeDtypeStruct(block, jnp.bfloat16),
        in_specs=[vmem] * 2,
        out_specs=vmem,
        scratch_shapes=[
            pltpu.VMEM((n_row, groups, rows, pack * cols), jnp.bfloat16),
            pltpu.VMEM((groups, pack * rows, pack * cols), jnp.bfloat16),
            pltpu.VMEM((n_col,) + block, jnp.bfloat16),
            pltpu.VMEM((n_col + 1,) + block, jnp.bfloat16),
            dma,
            dma((n_row.bit_length() - 1, n_row, CHUNKS)),
            dma((n_row, CHUNKS)),
            dma((n_col, CHUNKS)),
            dma((n_col, CHUNKS)),
            dma((n_col + 1, CHUNKS)),
        ],
        compiler_params=pltpu.CompilerParams(
            collective_id=2, has_side_effects=True, vmem_limit_bytes=58 * 2**20
        ),
        name="triangle",
    )(packed(left), packed(right))
    return (
        summed.reshape(groups, cols, pack, rows).transpose(3, 1, 2, 0).reshape(rows, cols, channels)
    )


def attend_kernel(
    n_row,
    n_col,
    n_heads,
    normed_ref,
    bias_ref,
    pair_ref,
    wq_ref,
    wk_ref,
    wvt_ref,
    wg_ref,
    wo_ref,
    out_ref,
    blocks,
    land,
    bias_all,
    bias_full,
    q_wide,
    top,
    total,
    acc,
    hop1_send,
    hop1_recv,
    hop2_send,
    hop2_recv,
    hop3_send,
    hop3_recv,
    copy_sem,
    right_send,
    left_send,
    block_recv,
):
    row = lax.axis_index("row")
    col = lax.axis_index("col")
    rows, cols, channels = normed_ref.shape
    halves = cols // rows
    head = channels // n_heads
    wide = cols * n_heads
    strip = rows * n_heads
    core = lax.rem(row, halves)
    home = row // halves
    groups = n_row // halves
    part = rows // PIECES

    barrier = pltpu.get_barrier_semaphore()
    for step in range(1, n_row):
        pl.semaphore_signal(
            barrier, inc=1, device_id=(lax.rem(row + step, n_row), col), device_id_type=MESH
        )
    for step in range(1, n_col):
        pl.semaphore_signal(
            barrier, inc=1, device_id=(row, lax.rem(col + step, n_col)), device_id_type=MESH
        )
    pl.semaphore_wait(barrier, n_row - 1 + n_col - 1)

    def hop1(source):
        return pltpu.make_async_remote_copy(
            src_ref=bias_ref,
            dst_ref=land.at[source],
            send_sem=hop1_send,
            recv_sem=hop1_recv.at[source],
            device_id=(row, home),
            device_id_type=MESH,
        )

    @pl.when(col != home)
    def _():
        hop1(col).start()

    def piece_copy(owner, piece, own, to_right):
        at = pl.ds(piece * part, part)
        source = normed_ref.at[at] if own else blocks.at[owner, at]
        sems = right_send if to_right else left_send
        return pltpu.make_async_remote_copy(
            src_ref=source,
            dst_ref=blocks.at[owner, at],
            send_sem=sems.at[owner, piece],
            recv_sem=block_recv.at[owner, piece],
            device_id=(row, col + 1 if to_right else col - 1),
            device_id_type=MESH,
        )

    for piece in range(PIECES):

        @pl.when(col < n_col - 1)
        def _():
            piece_copy(col, piece, True, True).start()

        @pl.when(col > 0)
        def _():
            piece_copy(col, piece, True, False).start()

    lane = lax.broadcasted_iota(jnp.int32, (rows, channels), 1) // head

    def make_queries(i, carry):
        query = jnp.dot(normed_ref[i], wq_ref[...], preferred_element_type=jnp.float32)
        for half in range(halves):
            mine = query[half * rows : (half + 1) * rows]
            for h in range(n_heads):
                start = half * strip + h * rows
                q_wide[i, start : start + rows, :] = jnp.where(lane == h, mine, 0.0).astype(
                    jnp.bfloat16
                )
        return carry

    lax.fori_loop(0, rows, make_queries, 0, unroll=2)

    def hop2(step):
        return pltpu.make_async_remote_copy(
            src_ref=land,
            dst_ref=bias_all.at[core],
            send_sem=hop2_send.at[step],
            recv_sem=hop2_recv,
            device_id=(lax.rem(home + step, groups) * halves + core, col),
            device_id_type=MESH,
        )

    def hop3(slot):
        return pltpu.make_async_remote_copy(
            src_ref=bias_all.at[slot],
            dst_ref=bias_all.at[slot],
            send_sem=hop3_send,
            recv_sem=hop3_recv,
            device_id=(home * halves + (1 - core), col),
            device_id_type=MESH,
        )

    @pl.when(col == home)
    def _():
        own = pltpu.make_async_copy(bias_ref, land.at[col], copy_sem)
        own.start()
        own.wait()
        for step in range(1, n_col):
            hop1(lax.rem(col + step, n_col)).wait_recv()
        for step in range(1, groups):
            hop2(step).start()
        keep = pltpu.make_async_copy(land, bias_all.at[core], copy_sem)
        keep.start()
        keep.wait()

    @pl.when(col != home)
    def _():
        hop2(1).wait_recv()

    hop3(core).start()
    hop3(1 - core).wait_recv()

    for k in range(n_col):
        for half in range(halves):
            bias_full[k, :, half * strip : (half + 1) * strip] = (
                bias_all[half, k].astype(jnp.float32) * LOG2E
            )

    lane_head = lax.rem(lax.broadcasted_iota(jnp.int32, (head, wide), 1), strip) // rows
    factor = LOG2E / math.sqrt(head)

    def attend(block, owner, i, first):
        keys = jnp.dot(block, wk_ref[...], preferred_element_type=jnp.float32).astype(jnp.bfloat16)
        values = contract_last(wvt_ref[...], block).astype(jnp.bfloat16)
        scores = contract_last(keys, q_wide[i]) * factor + bias_full[owner]
        peak = jnp.max(scores, axis=0, keepdims=True)
        if not first:
            old = top[i]
            peak = jnp.maximum(old, peak)
            shrink = jnp.exp2(old - peak)
        expo = jnp.exp2(scores - peak)
        summed = jnp.sum(expo, axis=0, keepdims=True)
        mixed = jnp.dot(values, expo.astype(jnp.bfloat16), preferred_element_type=jnp.float32)
        picked = mixed[:head]
        for h in range(1, n_heads):
            picked = jnp.where(lane_head == h, mixed[h * head : (h + 1) * head], picked)
        top[i] = peak
        if first:
            total[i] = summed
            acc[i] = picked
        else:
            total[i] = total[i] * shrink + summed
            acc[i] = acc[i] * shrink + picked

    def own_rows(i, carry):
        attend(normed_ref[i], col, i, True)
        return carry

    lax.fori_loop(0, rows, own_rows, 0, unroll=2)

    def arrived(step, carry):
        low, high = col - step, col + step
        for piece in range(PIECES):

            def rows_of(owner):
                def one(n, carry):
                    i = piece * part + n
                    attend(blocks[owner, i], owner, i, False)
                    return carry

                lax.fori_loop(0, part, one, 0, unroll=2)

            @pl.when(low >= 0)
            def _():
                piece_copy(low, piece, False, True).wait_recv()

                @pl.when(col < n_col - 1)
                def _():
                    piece_copy(low, piece, False, True).start()

            @pl.when(high < n_col)
            def _():
                piece_copy(high, piece, False, False).wait_recv()

                @pl.when(col > 0)
                def _():
                    piece_copy(high, piece, False, False).start()

            @pl.when(low >= 0)
            def _():
                rows_of(low)

            @pl.when(high < n_col)
            def _():
                rows_of(high)

        return carry

    lax.fori_loop(1, n_col, arrived, 0)

    def finish(i, carry):
        gate = jax.nn.sigmoid(
            jnp.dot(normed_ref[i], wg_ref[...], preferred_element_type=jnp.float32)
        )
        mean = acc[i] / total[i]
        stacked = jnp.concatenate(
            [
                jnp.concatenate(
                    [
                        mean[:, half * strip + h * rows : half * strip + (h + 1) * rows]
                        for half in range(halves)
                    ],
                    axis=1,
                )
                for h in range(n_heads)
            ],
            axis=0,
        )
        gated = (gate * stacked.T).astype(jnp.bfloat16)
        out_ref[i] = (
            pair_ref[i].astype(jnp.float32)
            + jnp.dot(gated, wo_ref[...], preferred_element_type=jnp.float32)
        ).astype(jnp.bfloat16)
        return carry

    lax.fori_loop(0, rows, finish, 0, unroll=2)

    @pl.when(col != home)
    def _():
        hop1(col).wait_send()

    @pl.when(col == home)
    def _():
        for step in range(1, groups):
            hop2(step).wait_send()

    hop3(core).wait_send()
    for piece in range(PIECES):
        for owner in range(n_col):

            @pl.when((owner <= col) & (col < n_col - 1))
            def _():
                piece_copy(owner, piece, False, True).wait_send()

            @pl.when((owner >= col) & (col > 0))
            def _():
                piece_copy(owner, piece, False, False).wait_send()


def attend(n_row, n_col, n_heads, normed, bias, pair, wq, wk, wvt, wg, wo):
    rows, cols, channels = normed.shape
    halves = cols // rows
    assert halves == 2 and cols % rows == 0 and n_row % 2 == 0
    groups = n_row // halves
    wide = cols * n_heads
    dma = pltpu.SemaphoreType.DMA
    vmem = pl.BlockSpec(memory_space=pltpu.VMEM)
    return pl.pallas_call(
        functools.partial(attend_kernel, n_row, n_col, n_heads),
        out_shape=jax.ShapeDtypeStruct(normed.shape, jnp.bfloat16),
        in_specs=[vmem] * 8,
        out_specs=vmem,
        scratch_shapes=[
            pltpu.VMEM((n_col,) + normed.shape, jnp.bfloat16),
            pltpu.VMEM((n_col,) + bias.shape, jnp.bfloat16),
            pltpu.VMEM((halves, n_col) + bias.shape, jnp.bfloat16),
            pltpu.VMEM((n_col, cols, wide), jnp.float32),
            pltpu.VMEM((rows, wide, channels), jnp.bfloat16),
            pltpu.VMEM((rows, 1, wide), jnp.float32),
            pltpu.VMEM((rows, 1, wide), jnp.float32),
            pltpu.VMEM((rows, channels // n_heads, wide), jnp.float32),
            dma,
            dma((n_col,)),
            dma((groups,)),
            dma,
            dma,
            dma,
            dma,
            dma((n_col, PIECES)),
            dma((n_col, PIECES)),
            dma((n_col, PIECES)),
        ],
        compiler_params=pltpu.CompilerParams(
            collective_id=1, has_side_effects=True, vmem_limit_bytes=48 * 2**20
        ),
        name="attend",
    )(normed, bias, pair, wq, wk, wvt, wg, wo)


def layer_norm(values, gain):
    center = values - jnp.mean(values, axis=-1, keepdims=True)
    spread = jnp.mean(center * center, axis=-1, keepdims=True)
    return center * lax.rsqrt(spread + 1e-05) * gain


def body(
    pair_in,
    coords,
    chain_ids,
    coord_mask,
    gain_tri,
    gain_sum,
    gain_attn,
    w_tri_in,
    w_tri_out,
    w_bins,
    same_chain,
    w_query,
    w_attn,
    w_bias,
    w_attn_out,
):
    row_count, col_count, channels = pair_in.shape
    n_heads = w_bias.shape[1]
    n_bins = w_bins.shape[0]
    col_start = lax.axis_index("col") * col_count
    coords_all, chains_all, masks_all = (
        lax.all_gather(coords, "row", axis=1, tiled=True),
        lax.all_gather(chain_ids, "row", axis=0, tiled=True),
        lax.all_gather(coord_mask, "row", axis=0, tiled=True),
    )
    pair_wide = pair_in.astype(jnp.float32)
    normed = layer_norm(pair_wide, gain_tri).astype(jnp.bfloat16)
    projected = jnp.dot(
        normed.reshape(row_count * col_count, channels),
        w_tri_in,
        preferred_element_type=jnp.float32,
    ).reshape(row_count, col_count, 5 * channels)
    left_side = (
        jax.nn.sigmoid(projected[..., :channels]) * projected[..., channels : 2 * channels]
    ).astype(jnp.bfloat16)
    right_side = (
        jax.nn.sigmoid(projected[..., 2 * channels : 3 * channels])
        * projected[..., 3 * channels : 4 * channels]
    ).astype(jnp.bfloat16)
    tri_gate = jax.nn.sigmoid(projected[..., 4 * channels :])
    product = triangle(lax.axis_size("row"), lax.axis_size("col"), left_side, right_side).astype(
        jnp.float32
    )
    summed_norm = layer_norm(product, gain_sum).astype(jnp.bfloat16)
    pair_one = pair_wide + tri_gate * jnp.dot(
        summed_norm.reshape(row_count * col_count, channels),
        w_tri_out,
        preferred_element_type=jnp.float32,
    ).reshape(row_count, col_count, channels)
    far_coords = lax.dynamic_slice_in_dim(coords_all, col_start, col_count, 1)
    far_chains = lax.dynamic_slice_in_dim(chains_all, col_start, col_count, 0)
    far_masks = lax.dynamic_slice_in_dim(masks_all, col_start, col_count, 0)
    offsets = coords[:, :, None] - far_coords[:, None, :]
    dist = jnp.sqrt(jnp.sum(offsets * offsets, axis=0) + 1.0)
    centres = 2.0 + 20.0 * jnp.arange(n_bins, dtype=jnp.float32) / (n_bins - 1)
    spacing = 25.0 / (n_bins - 1)
    pair_mask = coord_mask.astype(jnp.float32)[:, None] * far_masks.astype(jnp.float32)[None, :]
    feats = jnp.exp(-(((dist[..., None] - centres) / spacing) ** 2)) * pair_mask[..., None]
    binned = jnp.dot(
        feats.reshape(row_count * col_count, n_bins), w_bins, precision=lax.Precision.HIGHEST
    ).reshape(row_count, col_count, channels)
    shared = (chain_ids[:, None] == far_chains[None, :]).astype(jnp.float32)
    pair_two = (pair_one + binned + shared[..., None] * same_chain).astype(jnp.bfloat16)
    normed_two = layer_norm(pair_two.astype(jnp.float32), gain_attn).astype(jnp.bfloat16)
    flat_two = normed_two.reshape(row_count * col_count, channels)
    pair_bias = (
        jnp.dot(flat_two, w_bias, preferred_element_type=jnp.float32)
        .astype(jnp.bfloat16)
        .reshape(row_count, col_count, n_heads)
        .transpose(1, 2, 0)
        .reshape(col_count, n_heads * row_count)
    )
    return attend(
        lax.axis_size("row"),
        lax.axis_size("col"),
        n_heads,
        normed_two,
        pair_bias,
        pair_two,
        w_query,
        w_attn[:, :channels],
        w_attn[:, channels : 2 * channels].T,
        w_attn[:, 2 * channels :],
        w_attn_out,
    )


def solution(mesh):
    return jax.shard_map(
        body,
        mesh=mesh,
        in_specs=(
            P("row", "col", None),
            P(None, "row"),
            P("row"),
            P("row"),
            P(),
            P(),
            P(),
            P(),
            P(),
            P(),
            P(),
            P(),
            P(),
            P(),
            P(),
        ),
        out_specs=P("row", "col", None),
        check_vma=False,
    )
```

```python
import functools
import math

import jax
import jax.numpy as jnp
from jax import lax
from jax.experimental import pallas as pl
from jax.experimental.pallas import tpu as pltpu
from jax.sharding import PartitionSpec as P

MESH = pl.DeviceIdType.MESH
LOG2E = math.log2(math.e)
PIECES = 2


def contract_last(a, b):
    return lax.dot_general(a, b, (((1,), (1,)), ((), ())), preferred_element_type=jnp.float32)


CHUNKS = 4


def flip(index, bit):
    return index + bit - 2 * bit * lax.rem(index // bit, 2)


def routes(bits):
    found = []
    for offset in range(2, sum(bits) + 2, 2):
        used = [n for n, bit in enumerate(bits) if offset & bit]
        found.append((len(used), offset, bits[used[-1] + 1 :]))
    return [(offset, later) for _, offset, later in sorted(found)]


def triangle_kernel(
    n_row,
    n_col,
    pack,
    left_ref,
    right_ref,
    facts_ref,
    out_ref,
    facts_out,
    gathered,
    facts,
    facts_send,
    facts_recv,
    left_wide,
    sums,
    land,
    own_sem,
    hop_send,
    hop_recv,
    up_send,
    down_send,
    sum_recv,
):
    row = lax.axis_index("row")
    col = lax.axis_index("col")
    groups, rows, depth = left_ref.shape
    chunk = groups // CHUNKS
    cols = depth // pack
    halves = cols // rows
    core = lax.rem(row, 2)
    bits = [1 << n for n in range(1, n_row.bit_length() - 1)]
    orders = (bits, bits[::-1])

    barrier = pltpu.get_barrier_semaphore()
    for step in range(1, n_row):
        pl.semaphore_signal(
            barrier, inc=1, device_id=(lax.rem(row + step, n_row), col), device_id_type=MESH
        )
    for step in range(1, n_col):
        pl.semaphore_signal(
            barrier, inc=1, device_id=(row, lax.rem(col + step, n_col)), device_id_type=MESH
        )
    pl.semaphore_wait(barrier, n_row - 1 + n_col - 1)

    def hop(source, part, bit, own=False):
        at = pl.ds(part * chunk, chunk)
        return pltpu.make_async_remote_copy(
            src_ref=right_ref.at[at] if own else gathered.at[source, at],
            dst_ref=gathered.at[source, at],
            send_sem=hop_send.at[bit.bit_length() - 1, source, part],
            recv_sem=hop_recv.at[source, part],
            device_id=(flip(row, bit), col),
            device_id_type=MESH,
        )

    def tell(target, source):
        return pltpu.make_async_remote_copy(
            src_ref=facts_ref,
            dst_ref=facts.at[source],
            send_sem=facts_send.at[target],
            recv_sem=facts_recv.at[source],
            device_id=(target, col),
            device_id_type=MESH,
        )

    for step in range(1, n_row):
        tell(lax.rem(row + step, n_row), row).start()
    for part in range(CHUNKS):
        for bit in bits + [1]:
            hop(row, part, bit, True).start()
    own_copy = pltpu.make_async_copy(right_ref, gathered.at[row], own_sem)
    own_copy.start()

    lane = lax.broadcasted_iota(jnp.int32, (rows, depth), 1) // cols

    def widen(g, carry):
        mine = left_ref[g].astype(jnp.float32)
        for a in range(pack):
            left_wide[g, a * rows : (a + 1) * rows, :] = jnp.where(lane == a, mine, 0.0).astype(
                jnp.bfloat16
            )
        return carry

    lax.fori_loop(0, groups, widen, 0)
    own_copy.wait()

    def source_of(offset):
        source = row
        for bit in bits + [1]:
            if offset & bit:
                source = flip(source, bit)
        return source

    def forward(part):
        for parity in range(2):

            @pl.when(core == parity)
            def _():
                for offset, later in routes(orders[parity]):
                    source = source_of(offset)
                    hop(source, part, 1).wait_recv()
                    for bit in later + [1]:
                        hop(source, part, bit).start()

    def send_sum(dest, part, up):
        at = pl.ds(part * chunk, chunk)
        return pltpu.make_async_remote_copy(
            src_ref=sums.at[dest, at],
            dst_ref=land.at[dest + 1 if up else dest, at],
            send_sem=(up_send if up else down_send).at[dest, part],
            recv_sem=sum_recv.at[dest + 1 if up else dest, part],
            device_id=(row, col + 1 if up else col - 1),
            device_id_type=MESH,
        )

    def add_landed(dest, part, up):
        send_sum(dest, part, up).wait_recv()
        slot = dest + 1 if up else dest

        def one(n, carry):
            g = part * chunk + n
            sums[dest, g] = (
                sums[dest, g].astype(jnp.float32) + land[slot, g].astype(jnp.float32)
            ).astype(jnp.bfloat16)
            return carry

        lax.fori_loop(0, chunk, one, 0)

    def multiply(part):
        for offset in range(1, n_row, 2):
            hop(source_of(offset), part, 1).wait_recv()

        def partial(n, carry):
            g = part * chunk + n
            far = jnp.concatenate([gathered[source, g] for source in range(n_row)], axis=0)
            found = contract_last(far, left_wide[g]).astype(jnp.bfloat16)
            for dest in range(n_col):
                sums[dest, g] = found[dest * cols : (dest + 1) * cols]
            return carry

        lax.fori_loop(0, chunk, partial, 0)

        @pl.when(col == 0)
        def _():
            for dest in range(n_col - 1, 0, -1):
                send_sum(dest, part, True).start()

        @pl.when(col == n_col - 1)
        def _():
            for dest in range(n_col - 1):
                send_sum(dest, part, False).start()

        if part + 1 < CHUNKS:
            forward(part + 1)

    forward(0)
    multiply(0)
    for part in range(CHUNKS):
        if part + 1 < CHUNKS:
            multiply(part + 1)

        for step in range(1, n_col):
            high, low = n_col - step, step - 1

            @pl.when((col < high) & (col > 0))
            def _():
                add_landed(high, part, True)
                send_sum(high, part, True).start()

            @pl.when((col > low) & (col < n_col - 1))
            def _():
                add_landed(low, part, False)
                send_sum(low, part, False).start()

        @pl.when(col > 0)
        def _():
            add_landed(col, part, True)

        @pl.when(col < n_col - 1)
        def _():
            add_landed(col, part, False)

    def store(g, carry):
        out_ref[g] = sums[col, g]
        return carry

    lax.fori_loop(0, groups, store, 0)
    facts_out[row] = facts_ref[...]
    for step in range(1, n_row):
        source = lax.rem(row + step, n_row)
        tell(source, source).wait_recv()
        facts_out[source] = facts[source]
        tell(source, row).wait_send()

    for part in range(CHUNKS):
        for bit in bits + [1]:
            hop(row, part, bit, True).wait_send()
        for parity in range(2):

            @pl.when(core == parity)
            def _():
                for offset, later in routes(orders[parity]):
                    for bit in later + [1]:
                        hop(source_of(offset), part, bit).wait_send()

        for dest in range(n_col):

            @pl.when(col < dest)
            def _():
                send_sum(dest, part, True).wait_send()

            @pl.when(col > dest)
            def _():
                send_sum(dest, part, False).wait_send()


def triangle(n_row, n_col, left, right, facts):
    rows, cols, channels = left.shape
    pack = 128 // math.gcd(rows, 128)
    groups = channels // pack
    assert cols == 2 * rows and groups % CHUNKS == 0 and n_row & (n_row - 1) == 0

    def packed(side):
        return (
            side.reshape(rows, cols, pack, groups)
            .transpose(3, 0, 2, 1)
            .reshape(groups, rows, pack * cols)
        )

    dma = pltpu.SemaphoreType.DMA
    vmem = pl.BlockSpec(memory_space=pltpu.VMEM)
    block = (groups, cols, pack * rows)
    summed, facts_all = pl.pallas_call(
        functools.partial(triangle_kernel, n_row, n_col, pack),
        out_shape=[
            jax.ShapeDtypeStruct(block, jnp.bfloat16),
            jax.ShapeDtypeStruct((n_row,) + facts.shape, jnp.float32),
        ],
        in_specs=[vmem] * 3,
        out_specs=[vmem] * 2,
        scratch_shapes=[
            pltpu.VMEM((n_row, groups, rows, pack * cols), jnp.bfloat16),
            pltpu.VMEM((n_row,) + facts.shape, jnp.float32),
            dma((n_row,)),
            dma((n_row,)),
            pltpu.VMEM((groups, pack * rows, pack * cols), jnp.bfloat16),
            pltpu.VMEM((n_col,) + block, jnp.bfloat16),
            pltpu.VMEM((n_col + 1,) + block, jnp.bfloat16),
            dma,
            dma((n_row.bit_length() - 1, n_row, CHUNKS)),
            dma((n_row, CHUNKS)),
            dma((n_col, CHUNKS)),
            dma((n_col, CHUNKS)),
            dma((n_col + 1, CHUNKS)),
        ],
        compiler_params=pltpu.CompilerParams(
            collective_id=2, has_side_effects=True, vmem_limit_bytes=58 * 2**20
        ),
        name="triangle",
    )(packed(left), packed(right), facts)
    product = (
        summed.reshape(groups, cols, pack, rows).transpose(3, 1, 2, 0).reshape(rows, cols, channels)
    )
    return product, facts_all[:, :, :rows].transpose(1, 0, 2).reshape(facts.shape[0], -1)


def attend_kernel(
    n_row,
    n_col,
    n_heads,
    normed_ref,
    bias_ref,
    pair_ref,
    wq_ref,
    wk_ref,
    wvt_ref,
    wg_ref,
    wo_ref,
    out_ref,
    blocks,
    land,
    bias_all,
    bias_full,
    q_wide,
    top,
    total,
    acc,
    hop1_send,
    hop1_recv,
    hop2_send,
    hop2_recv,
    hop3_send,
    hop3_recv,
    copy_sem,
    right_send,
    left_send,
    block_recv,
):
    row = lax.axis_index("row")
    col = lax.axis_index("col")
    rows, cols, channels = normed_ref.shape
    halves = cols // rows
    head = channels // n_heads
    wide = cols * n_heads
    strip = rows * n_heads
    core = lax.rem(row, halves)
    home = row // halves
    groups = n_row // halves
    part = rows // PIECES

    barrier = pltpu.get_barrier_semaphore()
    for step in range(1, n_row):
        pl.semaphore_signal(
            barrier, inc=1, device_id=(lax.rem(row + step, n_row), col), device_id_type=MESH
        )
    for step in range(1, n_col):
        pl.semaphore_signal(
            barrier, inc=1, device_id=(row, lax.rem(col + step, n_col)), device_id_type=MESH
        )
    pl.semaphore_wait(barrier, n_row - 1 + n_col - 1)

    def hop1(source):
        return pltpu.make_async_remote_copy(
            src_ref=bias_ref,
            dst_ref=land.at[source],
            send_sem=hop1_send,
            recv_sem=hop1_recv.at[source],
            device_id=(row, home),
            device_id_type=MESH,
        )

    @pl.when(col != home)
    def _():
        hop1(col).start()

    def piece_copy(owner, piece, own, to_right):
        at = pl.ds(piece * part, part)
        source = normed_ref.at[at] if own else blocks.at[owner, at]
        sems = right_send if to_right else left_send
        return pltpu.make_async_remote_copy(
            src_ref=source,
            dst_ref=blocks.at[owner, at],
            send_sem=sems.at[owner, piece],
            recv_sem=block_recv.at[owner, piece],
            device_id=(row, col + 1 if to_right else col - 1),
            device_id_type=MESH,
        )

    for piece in range(PIECES):

        @pl.when(col < n_col - 1)
        def _():
            piece_copy(col, piece, True, True).start()

        @pl.when(col > 0)
        def _():
            piece_copy(col, piece, True, False).start()

    lane = lax.broadcasted_iota(jnp.int32, (rows, channels), 1) // head

    def make_queries(i, carry):
        query = jnp.dot(normed_ref[i], wq_ref[...], preferred_element_type=jnp.float32)
        for half in range(halves):
            mine = query[half * rows : (half + 1) * rows]
            for h in range(n_heads):
                start = half * strip + h * rows
                q_wide[i, start : start + rows, :] = jnp.where(lane == h, mine, 0.0).astype(
                    jnp.bfloat16
                )
        return carry

    lax.fori_loop(0, rows, make_queries, 0, unroll=2)

    def hop2(step):
        return pltpu.make_async_remote_copy(
            src_ref=land,
            dst_ref=bias_all.at[core],
            send_sem=hop2_send.at[step],
            recv_sem=hop2_recv,
            device_id=(lax.rem(home + step, groups) * halves + core, col),
            device_id_type=MESH,
        )

    def hop3(slot):
        return pltpu.make_async_remote_copy(
            src_ref=bias_all.at[slot],
            dst_ref=bias_all.at[slot],
            send_sem=hop3_send,
            recv_sem=hop3_recv,
            device_id=(home * halves + (1 - core), col),
            device_id_type=MESH,
        )

    @pl.when(col == home)
    def _():
        own = pltpu.make_async_copy(bias_ref, land.at[col], copy_sem)
        own.start()
        own.wait()
        for step in range(1, n_col):
            hop1(lax.rem(col + step, n_col)).wait_recv()
        for step in range(1, groups):
            hop2(step).start()
        keep = pltpu.make_async_copy(land, bias_all.at[core], copy_sem)
        keep.start()
        keep.wait()

    @pl.when(col != home)
    def _():
        hop2(1).wait_recv()

    hop3(core).start()
    hop3(1 - core).wait_recv()

    for k in range(n_col):
        for half in range(halves):
            bias_full[k, :, half * strip : (half + 1) * strip] = (
                bias_all[half, k].astype(jnp.float32) * LOG2E
            )

    lane_head = lax.rem(lax.broadcasted_iota(jnp.int32, (head, wide), 1), strip) // rows
    factor = LOG2E / math.sqrt(head)

    def attend(block, owner, i, first):
        keys = jnp.dot(block, wk_ref[...], preferred_element_type=jnp.float32).astype(jnp.bfloat16)
        values = contract_last(wvt_ref[...], block).astype(jnp.bfloat16)
        scores = contract_last(keys, q_wide[i]) * factor + bias_full[owner]
        peak = jnp.max(scores, axis=0, keepdims=True)
        if not first:
            old = top[i]
            peak = jnp.maximum(old, peak)
            shrink = jnp.exp2(old - peak)
        expo = jnp.exp2(scores - peak)
        summed = jnp.sum(expo, axis=0, keepdims=True)
        mixed = jnp.dot(values, expo.astype(jnp.bfloat16), preferred_element_type=jnp.float32)
        picked = mixed[:head]
        for h in range(1, n_heads):
            picked = jnp.where(lane_head == h, mixed[h * head : (h + 1) * head], picked)
        top[i] = peak
        if first:
            total[i] = summed
            acc[i] = picked
        else:
            total[i] = total[i] * shrink + summed
            acc[i] = acc[i] * shrink + picked

    def own_rows(i, carry):
        attend(normed_ref[i], col, i, True)
        return carry

    lax.fori_loop(0, rows, own_rows, 0, unroll=2)

    def arrived(step, carry):
        low, high = col - step, col + step
        for piece in range(PIECES):

            def rows_of(owner):
                def one(n, carry):
                    i = piece * part + n
                    attend(blocks[owner, i], owner, i, False)
                    return carry

                lax.fori_loop(0, part, one, 0, unroll=2)

            @pl.when(low >= 0)
            def _():
                piece_copy(low, piece, False, True).wait_recv()

                @pl.when(col < n_col - 1)
                def _():
                    piece_copy(low, piece, False, True).start()

            @pl.when(high < n_col)
            def _():
                piece_copy(high, piece, False, False).wait_recv()

                @pl.when(col > 0)
                def _():
                    piece_copy(high, piece, False, False).start()

            @pl.when(low >= 0)
            def _():
                rows_of(low)

            @pl.when(high < n_col)
            def _():
                rows_of(high)

        return carry

    lax.fori_loop(1, n_col, arrived, 0)

    def finish(i, carry):
        gate = jax.nn.sigmoid(
            jnp.dot(normed_ref[i], wg_ref[...], preferred_element_type=jnp.float32)
        )
        mean = acc[i] / total[i]
        stacked = jnp.concatenate(
            [
                jnp.concatenate(
                    [
                        mean[:, half * strip + h * rows : half * strip + (h + 1) * rows]
                        for half in range(halves)
                    ],
                    axis=1,
                )
                for h in range(n_heads)
            ],
            axis=0,
        )
        gated = (gate * stacked.T).astype(jnp.bfloat16)
        out_ref[i] = (
            pair_ref[i].astype(jnp.float32)
            + jnp.dot(gated, wo_ref[...], preferred_element_type=jnp.float32)
        ).astype(jnp.bfloat16)
        return carry

    lax.fori_loop(0, rows, finish, 0, unroll=2)

    @pl.when(col != home)
    def _():
        hop1(col).wait_send()

    @pl.when(col == home)
    def _():
        for step in range(1, groups):
            hop2(step).wait_send()

    hop3(core).wait_send()
    for piece in range(PIECES):
        for owner in range(n_col):

            @pl.when((owner <= col) & (col < n_col - 1))
            def _():
                piece_copy(owner, piece, False, True).wait_send()

            @pl.when((owner >= col) & (col > 0))
            def _():
                piece_copy(owner, piece, False, False).wait_send()


def attend(n_row, n_col, n_heads, normed, bias, pair, wq, wk, wvt, wg, wo):
    rows, cols, channels = normed.shape
    halves = cols // rows
    assert halves == 2 and cols % rows == 0 and n_row % 2 == 0
    groups = n_row // halves
    wide = cols * n_heads
    dma = pltpu.SemaphoreType.DMA
    vmem = pl.BlockSpec(memory_space=pltpu.VMEM)
    return pl.pallas_call(
        functools.partial(attend_kernel, n_row, n_col, n_heads),
        out_shape=jax.ShapeDtypeStruct(normed.shape, jnp.bfloat16),
        in_specs=[vmem] * 8,
        out_specs=vmem,
        scratch_shapes=[
            pltpu.VMEM((n_col,) + normed.shape, jnp.bfloat16),
            pltpu.VMEM((n_col,) + bias.shape, jnp.bfloat16),
            pltpu.VMEM((halves, n_col) + bias.shape, jnp.bfloat16),
            pltpu.VMEM((n_col, cols, wide), jnp.float32),
            pltpu.VMEM((rows, wide, channels), jnp.bfloat16),
            pltpu.VMEM((rows, 1, wide), jnp.float32),
            pltpu.VMEM((rows, 1, wide), jnp.float32),
            pltpu.VMEM((rows, channels // n_heads, wide), jnp.float32),
            dma,
            dma((n_col,)),
            dma((groups,)),
            dma,
            dma,
            dma,
            dma,
            dma((n_col, PIECES)),
            dma((n_col, PIECES)),
            dma((n_col, PIECES)),
        ],
        compiler_params=pltpu.CompilerParams(
            collective_id=1, has_side_effects=True, vmem_limit_bytes=48 * 2**20
        ),
        name="attend",
    )(normed, bias, pair, wq, wk, wvt, wg, wo)


def layer_norm(values, gain):
    center = values - jnp.mean(values, axis=-1, keepdims=True)
    spread = jnp.mean(center * center, axis=-1, keepdims=True)
    return center * lax.rsqrt(spread + 1e-05) * gain


def body(
    pair_in,
    coords,
    chain_ids,
    coord_mask,
    gain_tri,
    gain_sum,
    gain_attn,
    w_tri_in,
    w_tri_out,
    w_bins,
    same_chain,
    w_query,
    w_attn,
    w_bias,
    w_attn_out,
):
    row_count, col_count, channels = pair_in.shape
    n_heads = w_bias.shape[1]
    n_bins = w_bins.shape[0]
    col_start = lax.axis_index("col") * col_count
    facts = jnp.concatenate(
        [
            coords,
            chain_ids.astype(jnp.float32)[None],
            coord_mask.astype(jnp.float32)[None],
        ],
        axis=0,
    )
    facts = jnp.pad(facts, ((0, -facts.shape[0] % 8), (0, -row_count % 128)))
    pair_wide = pair_in.astype(jnp.float32)
    normed = layer_norm(pair_wide, gain_tri).astype(jnp.bfloat16)
    projected = jnp.dot(
        normed.reshape(row_count * col_count, channels),
        w_tri_in,
        preferred_element_type=jnp.float32,
    ).reshape(row_count, col_count, 5 * channels)
    left_side = (
        jax.nn.sigmoid(projected[..., :channels]) * projected[..., channels : 2 * channels]
    ).astype(jnp.bfloat16)
    right_side = (
        jax.nn.sigmoid(projected[..., 2 * channels : 3 * channels])
        * projected[..., 3 * channels : 4 * channels]
    ).astype(jnp.bfloat16)
    tri_gate = jax.nn.sigmoid(projected[..., 4 * channels :])
    product, facts_all = triangle(
        lax.axis_size("row"), lax.axis_size("col"), left_side, right_side, facts
    )
    product = product.astype(jnp.float32)
    summed_norm = layer_norm(product, gain_sum).astype(jnp.bfloat16)
    pair_one = pair_wide + tri_gate * jnp.dot(
        summed_norm.reshape(row_count * col_count, channels),
        w_tri_out,
        preferred_element_type=jnp.float32,
    ).reshape(row_count, col_count, channels)
    far_facts = lax.dynamic_slice_in_dim(facts_all, col_start, col_count, 1)
    far_coords, far_chains, far_masks = far_facts[:3], far_facts[3], far_facts[4]
    offsets = coords[:, :, None] - far_coords[:, None, :]
    dist = jnp.sqrt(jnp.sum(offsets * offsets, axis=0) + 1.0)
    centres = 2.0 + 20.0 * jnp.arange(n_bins, dtype=jnp.float32) / (n_bins - 1)
    spacing = 25.0 / (n_bins - 1)
    pair_mask = coord_mask.astype(jnp.float32)[:, None] * far_masks[None, :]
    feats = jnp.exp(-(((dist[..., None] - centres) / spacing) ** 2)) * pair_mask[..., None]
    binned = jnp.dot(
        feats.reshape(row_count * col_count, n_bins), w_bins, precision=lax.Precision.HIGHEST
    ).reshape(row_count, col_count, channels)
    shared = (chain_ids.astype(jnp.float32)[:, None] == far_chains[None, :]).astype(jnp.float32)
    pair_two = (pair_one + binned + shared[..., None] * same_chain).astype(jnp.bfloat16)
    normed_two = layer_norm(pair_two.astype(jnp.float32), gain_attn).astype(jnp.bfloat16)
    flat_two = normed_two.reshape(row_count * col_count, channels)
    pair_bias = (
        jnp.dot(flat_two, w_bias, preferred_element_type=jnp.float32)
        .astype(jnp.bfloat16)
        .reshape(row_count, col_count, n_heads)
        .transpose(1, 2, 0)
        .reshape(col_count, n_heads * row_count)
    )
    return attend(
        lax.axis_size("row"),
        lax.axis_size("col"),
        n_heads,
        normed_two,
        pair_bias,
        pair_two,
        w_query,
        w_attn[:, :channels],
        w_attn[:, channels : 2 * channels].T,
        w_attn[:, 2 * channels :],
        w_attn_out,
    )


def solution(mesh):
    return jax.shard_map(
        body,
        mesh=mesh,
        in_specs=(
            P("row", "col", None),
            P(None, "row"),
            P("row"),
            P("row"),
            P(),
            P(),
            P(),
            P(),
            P(),
            P(),
            P(),
            P(),
            P(),
            P(),
            P(),
        ),
        out_specs=P("row", "col", None),
        check_vma=False,
    )
```

```python
import functools
import math

import jax
import jax.numpy as jnp
from jax import lax
from jax.experimental import pallas as pl
from jax.experimental.pallas import tpu as pltpu
from jax.sharding import PartitionSpec as P

MESH = pl.DeviceIdType.MESH
LOG2E = math.log2(math.e)
PIECES = 2


def contract_last(a, b):
    return lax.dot_general(a, b, (((1,), (1,)), ((), ())), preferred_element_type=jnp.float32)


CHUNKS = 4


def flip(index, bit):
    return index + bit - 2 * bit * lax.rem(index // bit, 2)


def routes(bits):
    found = []
    for offset in range(2, sum(bits) + 2, 2):
        used = [n for n, bit in enumerate(bits) if offset & bit]
        found.append((len(used), offset, bits[used[-1] + 1 :]))
    return [(offset, later) for _, offset, later in sorted(found)]


def triangle_kernel(
    n_row,
    n_col,
    pack,
    left_ref,
    right_ref,
    facts_ref,
    out_ref,
    facts_out,
    gathered,
    facts,
    facts_send,
    facts_recv,
    left_wide,
    sums,
    land,
    own_sem,
    hop_send,
    hop_recv,
    up_send,
    down_send,
    sum_recv,
):
    row = lax.axis_index("row")
    col = lax.axis_index("col")
    groups, rows, depth = left_ref.shape
    chunk = groups // CHUNKS
    cols = depth // pack
    halves = cols // rows
    core = lax.rem(row, 2)
    bits = [1 << n for n in range(1, n_row.bit_length() - 1)]
    orders = (bits, bits[::-1])

    barrier = pltpu.get_barrier_semaphore()
    for step in range(1, n_row):
        pl.semaphore_signal(
            barrier, inc=1, device_id=(lax.rem(row + step, n_row), col), device_id_type=MESH
        )
    for step in range(1, n_col):
        pl.semaphore_signal(
            barrier, inc=1, device_id=(row, lax.rem(col + step, n_col)), device_id_type=MESH
        )
    pl.semaphore_wait(barrier, n_row - 1 + n_col - 1)

    def hop(source, part, bit, own=False):
        at = pl.ds(part * chunk, chunk)
        return pltpu.make_async_remote_copy(
            src_ref=right_ref.at[at] if own else gathered.at[source, at],
            dst_ref=gathered.at[source, at],
            send_sem=hop_send.at[bit.bit_length() - 1, source, part],
            recv_sem=hop_recv.at[source, part],
            device_id=(flip(row, bit), col),
            device_id_type=MESH,
        )

    def tell(target, source):
        return pltpu.make_async_remote_copy(
            src_ref=facts_ref,
            dst_ref=facts.at[source],
            send_sem=facts_send.at[target],
            recv_sem=facts_recv.at[source],
            device_id=(target, col),
            device_id_type=MESH,
        )

    for step in range(1, n_row):
        tell(lax.rem(row + step, n_row), row).start()
    for part in range(min(2, CHUNKS)):
        for bit in bits + [1]:
            hop(row, part, bit, True).start()
    own_copy = pltpu.make_async_copy(right_ref, gathered.at[row], own_sem)
    own_copy.start()

    lane = lax.broadcasted_iota(jnp.int32, (rows, depth), 1) // cols

    def widen(g, carry):
        mine = left_ref[g].astype(jnp.float32)
        for a in range(pack):
            left_wide[g, a * rows : (a + 1) * rows, :] = jnp.where(lane == a, mine, 0.0).astype(
                jnp.bfloat16
            )
        return carry

    lax.fori_loop(0, groups, widen, 0)
    own_copy.wait()

    def source_of(offset):
        source = row
        for bit in bits + [1]:
            if offset & bit:
                source = flip(source, bit)
        return source

    def forward(part):
        for parity in range(2):

            @pl.when(core == parity)
            def _():
                for offset, later in routes(orders[parity]):
                    source = source_of(offset)
                    hop(source, part, 1).wait_recv()
                    for bit in later + [1]:
                        hop(source, part, bit).start()

        if part + 2 < CHUNKS:
            for bit in bits + [1]:
                hop(row, part + 2, bit, True).start()

    def send_sum(dest, part, up):
        at = pl.ds(part * chunk, chunk)
        return pltpu.make_async_remote_copy(
            src_ref=sums.at[dest, at],
            dst_ref=land.at[dest + 1 if up else dest, at],
            send_sem=(up_send if up else down_send).at[dest, part],
            recv_sem=sum_recv.at[dest + 1 if up else dest, part],
            device_id=(row, col + 1 if up else col - 1),
            device_id_type=MESH,
        )

    def add_landed(dest, part, up):
        send_sum(dest, part, up).wait_recv()
        slot = dest + 1 if up else dest

        def one(n, carry):
            g = part * chunk + n
            sums[dest, g] = (
                sums[dest, g].astype(jnp.float32) + land[slot, g].astype(jnp.float32)
            ).astype(jnp.bfloat16)
            return carry

        lax.fori_loop(0, chunk, one, 0)

    def multiply(part):
        for offset in range(1, n_row, 2):
            hop(source_of(offset), part, 1).wait_recv()

        def partial(n, carry):
            g = part * chunk + n
            far = jnp.concatenate([gathered[source, g] for source in range(n_row)], axis=0)
            found = contract_last(far, left_wide[g]).astype(jnp.bfloat16)
            for dest in range(n_col):
                sums[dest, g] = found[dest * cols : (dest + 1) * cols]
            return carry

        lax.fori_loop(0, chunk, partial, 0)

        @pl.when(col == 0)
        def _():
            for dest in range(n_col - 1, 0, -1):
                send_sum(dest, part, True).start()

        @pl.when(col == n_col - 1)
        def _():
            for dest in range(n_col - 1):
                send_sum(dest, part, False).start()

        if part + 1 < CHUNKS:
            forward(part + 1)

    forward(0)
    multiply(0)
    for part in range(CHUNKS):
        if part + 1 < CHUNKS:
            multiply(part + 1)

        for step in range(1, n_col):
            high, low = n_col - step, step - 1

            @pl.when((col < high) & (col > 0))
            def _():
                add_landed(high, part, True)
                send_sum(high, part, True).start()

            @pl.when((col > low) & (col < n_col - 1))
            def _():
                add_landed(low, part, False)
                send_sum(low, part, False).start()

        @pl.when(col > 0)
        def _():
            add_landed(col, part, True)

        @pl.when(col < n_col - 1)
        def _():
            add_landed(col, part, False)

    def store(g, carry):
        out_ref[g] = sums[col, g]
        return carry

    lax.fori_loop(0, groups, store, 0)
    facts_out[row] = facts_ref[...]
    for step in range(1, n_row):
        source = lax.rem(row + step, n_row)
        tell(source, source).wait_recv()
        facts_out[source] = facts[source]
        tell(source, row).wait_send()

    for part in range(CHUNKS):
        for bit in bits + [1]:
            hop(row, part, bit, True).wait_send()
        for parity in range(2):

            @pl.when(core == parity)
            def _():
                for offset, later in routes(orders[parity]):
                    for bit in later + [1]:
                        hop(source_of(offset), part, bit).wait_send()

        for dest in range(n_col):

            @pl.when(col < dest)
            def _():
                send_sum(dest, part, True).wait_send()

            @pl.when(col > dest)
            def _():
                send_sum(dest, part, False).wait_send()


def triangle(n_row, n_col, left, right, facts):
    rows, cols, channels = left.shape
    pack = 128 // math.gcd(rows, 128)
    groups = channels // pack
    assert cols == 2 * rows and groups % CHUNKS == 0 and n_row & (n_row - 1) == 0

    def packed(side):
        return (
            side.reshape(rows, cols, pack, groups)
            .transpose(3, 0, 2, 1)
            .reshape(groups, rows, pack * cols)
        )

    dma = pltpu.SemaphoreType.DMA
    vmem = pl.BlockSpec(memory_space=pltpu.VMEM)
    block = (groups, cols, pack * rows)
    summed, facts_all = pl.pallas_call(
        functools.partial(triangle_kernel, n_row, n_col, pack),
        out_shape=[
            jax.ShapeDtypeStruct(block, jnp.bfloat16),
            jax.ShapeDtypeStruct((n_row,) + facts.shape, jnp.float32),
        ],
        in_specs=[vmem] * 3,
        out_specs=[vmem] * 2,
        scratch_shapes=[
            pltpu.VMEM((n_row, groups, rows, pack * cols), jnp.bfloat16),
            pltpu.VMEM((n_row,) + facts.shape, jnp.float32),
            dma((n_row,)),
            dma((n_row,)),
            pltpu.VMEM((groups, pack * rows, pack * cols), jnp.bfloat16),
            pltpu.VMEM((n_col,) + block, jnp.bfloat16),
            pltpu.VMEM((n_col + 1,) + block, jnp.bfloat16),
            dma,
            dma((n_row.bit_length() - 1, n_row, CHUNKS)),
            dma((n_row, CHUNKS)),
            dma((n_col, CHUNKS)),
            dma((n_col, CHUNKS)),
            dma((n_col + 1, CHUNKS)),
        ],
        compiler_params=pltpu.CompilerParams(
            collective_id=2, has_side_effects=True, vmem_limit_bytes=58 * 2**20
        ),
        name="triangle",
    )(packed(left), packed(right), facts)
    product = (
        summed.reshape(groups, cols, pack, rows).transpose(3, 1, 2, 0).reshape(rows, cols, channels)
    )
    return product, facts_all[:, :, :rows].transpose(1, 0, 2).reshape(facts.shape[0], -1)


def attend_kernel(
    n_row,
    n_col,
    n_heads,
    normed_ref,
    bias_ref,
    pair_ref,
    wq_ref,
    wk_ref,
    wvt_ref,
    wg_ref,
    wo_ref,
    out_ref,
    blocks,
    land,
    bias_all,
    bias_full,
    q_wide,
    top,
    total,
    acc,
    hop1_send,
    hop1_recv,
    hop2_send,
    hop2_recv,
    hop3_send,
    hop3_recv,
    copy_sem,
    right_send,
    left_send,
    block_recv,
):
    row = lax.axis_index("row")
    col = lax.axis_index("col")
    rows, cols, channels = normed_ref.shape
    halves = cols // rows
    head = channels // n_heads
    wide = cols * n_heads
    strip = rows * n_heads
    core = lax.rem(row, halves)
    home = row // halves
    groups = n_row // halves
    part = rows // PIECES

    barrier = pltpu.get_barrier_semaphore()
    for step in range(1, n_row):
        pl.semaphore_signal(
            barrier, inc=1, device_id=(lax.rem(row + step, n_row), col), device_id_type=MESH
        )
    for step in range(1, n_col):
        pl.semaphore_signal(
            barrier, inc=1, device_id=(row, lax.rem(col + step, n_col)), device_id_type=MESH
        )
    pl.semaphore_wait(barrier, n_row - 1 + n_col - 1)

    def hop1(source):
        return pltpu.make_async_remote_copy(
            src_ref=bias_ref,
            dst_ref=land.at[source],
            send_sem=hop1_send,
            recv_sem=hop1_recv.at[source],
            device_id=(row, home),
            device_id_type=MESH,
        )

    @pl.when(col != home)
    def _():
        hop1(col).start()

    def piece_copy(owner, piece, own, to_right):
        at = pl.ds(piece * part, part)
        source = normed_ref.at[at] if own else blocks.at[owner, at]
        sems = right_send if to_right else left_send
        return pltpu.make_async_remote_copy(
            src_ref=source,
            dst_ref=blocks.at[owner, at],
            send_sem=sems.at[owner, piece],
            recv_sem=block_recv.at[owner, piece],
            device_id=(row, col + 1 if to_right else col - 1),
            device_id_type=MESH,
        )

    for piece in range(PIECES):

        @pl.when(col < n_col - 1)
        def _():
            piece_copy(col, piece, True, True).start()

        @pl.when(col > 0)
        def _():
            piece_copy(col, piece, True, False).start()

    lane = lax.broadcasted_iota(jnp.int32, (rows, channels), 1) // head

    def make_queries(i, carry):
        query = jnp.dot(normed_ref[i], wq_ref[...], preferred_element_type=jnp.float32)
        for half in range(halves):
            mine = query[half * rows : (half + 1) * rows]
            for h in range(n_heads):
                start = half * strip + h * rows
                q_wide[i, start : start + rows, :] = jnp.where(lane == h, mine, 0.0).astype(
                    jnp.bfloat16
                )
        return carry

    lax.fori_loop(0, rows, make_queries, 0, unroll=2)

    def hop2(step):
        return pltpu.make_async_remote_copy(
            src_ref=land,
            dst_ref=bias_all.at[core],
            send_sem=hop2_send.at[step],
            recv_sem=hop2_recv,
            device_id=(lax.rem(home + step, groups) * halves + core, col),
            device_id_type=MESH,
        )

    def hop3(slot):
        return pltpu.make_async_remote_copy(
            src_ref=bias_all.at[slot],
            dst_ref=bias_all.at[slot],
            send_sem=hop3_send,
            recv_sem=hop3_recv,
            device_id=(home * halves + (1 - core), col),
            device_id_type=MESH,
        )

    @pl.when(col == home)
    def _():
        own = pltpu.make_async_copy(bias_ref, land.at[col], copy_sem)
        own.start()
        own.wait()
        for step in range(1, n_col):
            hop1(lax.rem(col + step, n_col)).wait_recv()
        for step in range(1, groups):
            hop2(step).start()
        keep = pltpu.make_async_copy(land, bias_all.at[core], copy_sem)
        keep.start()
        keep.wait()

    @pl.when(col != home)
    def _():
        hop2(1).wait_recv()

    hop3(core).start()
    hop3(1 - core).wait_recv()

    for k in range(n_col):
        for half in range(halves):
            bias_full[k, :, half * strip : (half + 1) * strip] = (
                bias_all[half, k].astype(jnp.float32) * LOG2E
            )

    lane_head = lax.rem(lax.broadcasted_iota(jnp.int32, (head, wide), 1), strip) // rows
    factor = LOG2E / math.sqrt(head)

    def attend(block, owner, i, first):
        keys = jnp.dot(block, wk_ref[...], preferred_element_type=jnp.float32).astype(jnp.bfloat16)
        values = contract_last(wvt_ref[...], block).astype(jnp.bfloat16)
        scores = contract_last(keys, q_wide[i]) * factor + bias_full[owner]
        peak = jnp.max(scores, axis=0, keepdims=True)
        if not first:
            old = top[i]
            peak = jnp.maximum(old, peak)
            shrink = jnp.exp2(old - peak)
        expo = jnp.exp2(scores - peak)
        summed = jnp.sum(expo, axis=0, keepdims=True)
        mixed = jnp.dot(values, expo.astype(jnp.bfloat16), preferred_element_type=jnp.float32)
        picked = mixed[:head]
        for h in range(1, n_heads):
            picked = jnp.where(lane_head == h, mixed[h * head : (h + 1) * head], picked)
        top[i] = peak
        if first:
            total[i] = summed
            acc[i] = picked
        else:
            total[i] = total[i] * shrink + summed
            acc[i] = acc[i] * shrink + picked

    def own_rows(i, carry):
        attend(normed_ref[i], col, i, True)
        return carry

    def pass_on(step, piece):
        low, high = col - step, col + step

        @pl.when(low >= 0)
        def _():
            piece_copy(low, piece, False, True).wait_recv()

            @pl.when(col < n_col - 1)
            def _():
                piece_copy(low, piece, False, True).start()

        @pl.when(high < n_col)
        def _():
            piece_copy(high, piece, False, False).wait_recv()

            @pl.when(col > 0)
            def _():
                piece_copy(high, piece, False, False).start()

    for piece in range(PIECES):
        pass_on(1, piece)

    lax.fori_loop(0, rows, own_rows, 0, unroll=2)

    def arrived(step, carry):
        low, high = col - step, col + step
        for piece in range(PIECES):

            def rows_of(owner):
                def one(n, carry):
                    i = piece * part + n
                    attend(blocks[owner, i], owner, i, False)
                    return carry

                lax.fori_loop(0, part, one, 0, unroll=2)

            @pl.when(step > 1)
            def _():
                pass_on(step, piece)

            @pl.when(low >= 0)
            def _():
                rows_of(low)

            @pl.when(high < n_col)
            def _():
                rows_of(high)

        return carry

    lax.fori_loop(1, n_col, arrived, 0)

    def finish(i, carry):
        gate = jax.nn.sigmoid(
            jnp.dot(normed_ref[i], wg_ref[...], preferred_element_type=jnp.float32)
        )
        mean = acc[i] / total[i]
        stacked = jnp.concatenate(
            [
                jnp.concatenate(
                    [
                        mean[:, half * strip + h * rows : half * strip + (h + 1) * rows]
                        for half in range(halves)
                    ],
                    axis=1,
                )
                for h in range(n_heads)
            ],
            axis=0,
        )
        gated = (gate * stacked.T).astype(jnp.bfloat16)
        out_ref[i] = (
            pair_ref[i].astype(jnp.float32)
            + jnp.dot(gated, wo_ref[...], preferred_element_type=jnp.float32)
        ).astype(jnp.bfloat16)
        return carry

    lax.fori_loop(0, rows, finish, 0, unroll=2)

    @pl.when(col != home)
    def _():
        hop1(col).wait_send()

    @pl.when(col == home)
    def _():
        for step in range(1, groups):
            hop2(step).wait_send()

    hop3(core).wait_send()
    for piece in range(PIECES):
        for owner in range(n_col):

            @pl.when((owner <= col) & (col < n_col - 1))
            def _():
                piece_copy(owner, piece, False, True).wait_send()

            @pl.when((owner >= col) & (col > 0))
            def _():
                piece_copy(owner, piece, False, False).wait_send()


def attend(n_row, n_col, n_heads, normed, bias, pair, wq, wk, wvt, wg, wo):
    rows, cols, channels = normed.shape
    halves = cols // rows
    assert halves == 2 and cols % rows == 0 and n_row % 2 == 0
    groups = n_row // halves
    wide = cols * n_heads
    dma = pltpu.SemaphoreType.DMA
    vmem = pl.BlockSpec(memory_space=pltpu.VMEM)
    return pl.pallas_call(
        functools.partial(attend_kernel, n_row, n_col, n_heads),
        out_shape=jax.ShapeDtypeStruct(normed.shape, jnp.bfloat16),
        in_specs=[vmem] * 8,
        out_specs=vmem,
        scratch_shapes=[
            pltpu.VMEM((n_col,) + normed.shape, jnp.bfloat16),
            pltpu.VMEM((n_col,) + bias.shape, jnp.bfloat16),
            pltpu.VMEM((halves, n_col) + bias.shape, jnp.bfloat16),
            pltpu.VMEM((n_col, cols, wide), jnp.float32),
            pltpu.VMEM((rows, wide, channels), jnp.bfloat16),
            pltpu.VMEM((rows, 1, wide), jnp.float32),
            pltpu.VMEM((rows, 1, wide), jnp.float32),
            pltpu.VMEM((rows, channels // n_heads, wide), jnp.float32),
            dma,
            dma((n_col,)),
            dma((groups,)),
            dma,
            dma,
            dma,
            dma,
            dma((n_col, PIECES)),
            dma((n_col, PIECES)),
            dma((n_col, PIECES)),
        ],
        compiler_params=pltpu.CompilerParams(
            collective_id=1, has_side_effects=True, vmem_limit_bytes=48 * 2**20
        ),
        name="attend",
    )(normed, bias, pair, wq, wk, wvt, wg, wo)


def layer_norm(values, gain):
    center = values - jnp.mean(values, axis=-1, keepdims=True)
    spread = jnp.mean(center * center, axis=-1, keepdims=True)
    return center * lax.rsqrt(spread + 1e-05) * gain


def body(
    pair_in,
    coords,
    chain_ids,
    coord_mask,
    gain_tri,
    gain_sum,
    gain_attn,
    w_tri_in,
    w_tri_out,
    w_bins,
    same_chain,
    w_query,
    w_attn,
    w_bias,
    w_attn_out,
):
    row_count, col_count, channels = pair_in.shape
    n_heads = w_bias.shape[1]
    n_bins = w_bins.shape[0]
    col_start = lax.axis_index("col") * col_count
    facts = jnp.concatenate(
        [
            coords,
            chain_ids.astype(jnp.float32)[None],
            coord_mask.astype(jnp.float32)[None],
        ],
        axis=0,
    )
    facts = jnp.pad(facts, ((0, -facts.shape[0] % 8), (0, -row_count % 128)))
    pair_wide = pair_in.astype(jnp.float32)
    normed = layer_norm(pair_wide, gain_tri).astype(jnp.bfloat16)
    projected = jnp.dot(
        normed.reshape(row_count * col_count, channels),
        w_tri_in,
        preferred_element_type=jnp.float32,
    ).reshape(row_count, col_count, 5 * channels)
    left_side = (
        jax.nn.sigmoid(projected[..., :channels]) * projected[..., channels : 2 * channels]
    ).astype(jnp.bfloat16)
    right_side = (
        jax.nn.sigmoid(projected[..., 2 * channels : 3 * channels])
        * projected[..., 3 * channels : 4 * channels]
    ).astype(jnp.bfloat16)
    tri_gate = jax.nn.sigmoid(projected[..., 4 * channels :])
    product, facts_all = triangle(
        lax.axis_size("row"), lax.axis_size("col"), left_side, right_side, facts
    )
    product = product.astype(jnp.float32)
    summed_norm = layer_norm(product, gain_sum).astype(jnp.bfloat16)
    pair_one = pair_wide + tri_gate * jnp.dot(
        summed_norm.reshape(row_count * col_count, channels),
        w_tri_out,
        preferred_element_type=jnp.float32,
    ).reshape(row_count, col_count, channels)
    far_facts = lax.dynamic_slice_in_dim(facts_all, col_start, col_count, 1)
    far_coords, far_chains, far_masks = far_facts[:3], far_facts[3], far_facts[4]
    offsets = coords[:, :, None] - far_coords[:, None, :]
    dist = jnp.sqrt(jnp.sum(offsets * offsets, axis=0) + 1.0)
    centres = 2.0 + 20.0 * jnp.arange(n_bins, dtype=jnp.float32) / (n_bins - 1)
    spacing = 25.0 / (n_bins - 1)
    pair_mask = coord_mask.astype(jnp.float32)[:, None] * far_masks[None, :]
    feats = jnp.exp(-(((dist[..., None] - centres) / spacing) ** 2)) * pair_mask[..., None]
    binned = jnp.dot(
        feats.reshape(row_count * col_count, n_bins), w_bins, precision=lax.Precision.HIGHEST
    ).reshape(row_count, col_count, channels)
    shared = (chain_ids.astype(jnp.float32)[:, None] == far_chains[None, :]).astype(jnp.float32)
    pair_two = (pair_one + binned + shared[..., None] * same_chain).astype(jnp.bfloat16)
    normed_two = layer_norm(pair_two.astype(jnp.float32), gain_attn).astype(jnp.bfloat16)
    flat_two = normed_two.reshape(row_count * col_count, channels)
    pair_bias = (
        jnp.dot(flat_two, w_bias, preferred_element_type=jnp.float32)
        .astype(jnp.bfloat16)
        .reshape(row_count, col_count, n_heads)
        .transpose(1, 2, 0)
        .reshape(col_count, n_heads * row_count)
    )
    return attend(
        lax.axis_size("row"),
        lax.axis_size("col"),
        n_heads,
        normed_two,
        pair_bias,
        pair_two,
        w_query,
        w_attn[:, :channels],
        w_attn[:, channels : 2 * channels].T,
        w_attn[:, 2 * channels :],
        w_attn_out,
    )


def solution(mesh):
    return jax.shard_map(
        body,
        mesh=mesh,
        in_specs=(
            P("row", "col", None),
            P(None, "row"),
            P("row"),
            P("row"),
            P(),
            P(),
            P(),
            P(),
            P(),
            P(),
            P(),
            P(),
            P(),
            P(),
            P(),
        ),
        out_specs=P("row", "col", None),
        check_vma=False,
    )
```
